32 devices in a mesh: pat: 8 (over y, x, core), feat: 4 (over z).
Axes of the slice: x: 2, y: 2, z: 4, core: 2. Of those that a mesh axis runs over, the one named last changes fastest.
Arguments:
- visits: bfloat16 [32768, 8192], P('pat', 'feat'), may hold values from -1.5 to 1.5
- counts: int32 [64], P('pat'), may hold values from 128 to 512, as said below
- patient_weight: float32 [64, 128], P('pat'), may hold values from 0.5 to 2
- phenotype_core: float32 [128, 128], replicated, may hold values from -0.5 to 0.5
- feature_factor: bfloat16 [8192, 128], P('feat'), may hold values from -0.0625 to 0.0625
- static_data: bfloat16 [64, 4096], P('pat', 'feat'), may hold values from -6 to 6
- static_factor: bfloat16 [4096, 128], P('feat'), may hold values from -0.09375 to 0.09375
Outputs:
- core_new: float32 [128, 128], replicated
- feature_new: float32 [8192, 128], P('feat')
- patient_new: float32 [64, 128], P('pat')
- static_new: float32 [4096, 128], P('feat')
The draws below stay inside these ranges and needn't reach their ends.
Inputs may be any that keep to these rules, and one draw needn't show every extreme that they name: `counts`: some patient of the last index of pat has exactly 512 visits.
All inputs are finite; a program needn't handle non-finite values.
Results may differ from the reference program's by a relative error of at most 0.0035.
Values may be sent and summed in bfloat16 or wider, within the bound.
A program may use at most 64 MiB of HBM per device.

```python
import math
import jax
import jax.numpy as jnp
from jax import lax

J = 8192
R = 128
P_SIZE = 4096
MAXV = 512
BLK = 128
SUB = 32
NS_STEPS = 8
PAT_DEV = 8
VIS_DEV = 4096
K = 64
VISITS = 32768
N_PAT = 8


def draw_counts(key, part):
    device_of = jnp.arange(K, dtype=jnp.int32) // PAT_DEV
    group_count = K // PAT_DEV
    upper_end = R + (MAXV - R) * (device_of + 1) // group_count
    drawn_counts = jax.random.randint(key, (K,), R, upper_end + 1, dtype=jnp.int32)
    full_spot = K - PAT_DEV + jax.random.randint(jax.random.fold_in(key, 7), (), 0, PAT_DEV, dtype=jnp.int32)
    return jnp.where(jnp.arange(K, dtype=jnp.int32) == full_spot, MAXV, drawn_counts).astype(jnp.int32)


def block_levels(own_key, dims, shards, least, top_value):
    level = 1.0
    for axis_at, blocks in shards:
        heights = jax.random.uniform(jax.random.fold_in(jax.random.fold_in(own_key, 6), axis_at), (blocks,), jnp.float32, least / len(shards), top_value / len(shards))
        level = level * jnp.repeat(jnp.exp(heights), dims[axis_at] // blocks).reshape((-1,) + (1,) * (len(dims) - 1 - axis_at))
    return level


def gaussian(stream_key, shape, spread, reach, cuts=(), held_as=jnp.bfloat16):
    values = jax.random.normal(stream_key, shape, jnp.float32) * spread
    if len(cuts) > 0:
        values = block_levels(stream_key, shape, cuts, -0.22, 0.18) * values
    return jnp.clip(values, min=-reach, max=reach).astype(held_as)


def setup_inputs(seed: int = 0) -> dict:
    arg_keys = jax.random.split(jax.random.key(seed), 8)
    visits = gaussian(arg_keys[0], (VISITS, J), 0.25, 1.5, ((0, 8), (1, 4)))
    counts = draw_counts(jax.random.fold_in(arg_keys[7], 71), 0)
    patient_weight = jnp.clip(jnp.exp(math.log(2.0) - 1.3862944 * jax.random.uniform(arg_keys[2], (K, R), jnp.float32) ** block_levels(arg_keys[2], (K, R), ((0, 8),), -0.2, 0.2)), 0.5, 2.0)
    phenotype_core = gaussian(arg_keys[3], (R, R), R ** -0.5, 0.5, (), jnp.float32)
    feature_factor = gaussian(arg_keys[4], (J, R), J ** -0.5, 0.0625, ((0, 4),))
    static_data = gaussian(arg_keys[5], (K, P_SIZE), 1.0, 6.0, ((0, 8), (1, 4)))
    static_factor = gaussian(arg_keys[6], (P_SIZE, R), P_SIZE ** -0.5, 0.09375, ((0, 4),))
    return {"visits": visits, "counts": counts, "patient_weight": patient_weight, "phenotype_core": phenotype_core, "feature_factor": feature_factor, "static_data": static_data, "static_factor": static_factor}


MU_RIDGE = 1.0

def layout(counts, rows, first):
    padded = (counts + BLK - 1) // BLK * BLK
    starts = jnp.cumsum(padded) - padded
    positions = first + jnp.arange(rows, dtype=jnp.int32)
    live = (positions[:, None] >= starts[None, :]) & (positions[:, None] < (starts + counts)[None, :])
    leading = positions[::SUB]
    member = (leading[:, None] >= starts[None, :]) & (leading[:, None] < (starts + padded)[None, :])
    return (live.astype(jnp.float32), member.astype(jnp.float32))

def contract_rows(left, right):
    return lax.dot_general(left, right, (((0,), (0,)), ((), ())), precision=lax.Precision.HIGHEST)

def core_field(projected, weight_rows, core):
    return lax.dot_general(projected * weight_rows, core, (((1,), (1,)), ((), ())), precision=lax.Precision.HIGHEST)

def block_grams(field, block_owner):
    pieces = field.reshape(-1, SUB, field.shape[1])
    grams = jnp.einsum('bvr,bvs->brs', pieces, pieces, precision=lax.Precision.HIGHEST)
    return jnp.einsum('bp,brs->prs', block_owner, grams, precision=lax.Precision.HIGHEST)

def batched(left, right):
    return jnp.einsum('nij,njk->nik', left, right, precision=lax.Precision.HIGHEST)

def polar_factor(grams):
    identity = jnp.eye(grams.shape[-1], dtype=jnp.float32)
    traces = jnp.trace(grams, axis1=1, axis2=2)
    moment = grams / traces[:, None, None]
    factor = identity[None] / jnp.sqrt(traces)[:, None, None]
    for iteration in range(NS_STEPS):
        correction = 1.5 * identity - 0.5 * moment
        factor = batched(factor, correction)
        moment = batched(batched(correction, moment), correction)
    return factor

def finish(field, projected, weight_rows, block_owner, row_owner, factor, core):
    rank = field.shape[1]
    block_factor = jnp.einsum('bp,prs->brs', block_owner, factor, precision=lax.Precision.HIGHEST)
    pieces = field.reshape(-1, SUB, rank)
    ortho = jnp.einsum('bvr,brs->bvs', pieces, block_factor, precision=lax.Precision.HIGHEST).reshape(-1, rank)
    mapped = jnp.dot(ortho, core, precision=lax.Precision.HIGHEST)
    patient_terms = contract_rows(row_owner, mapped * projected)
    core_terms = contract_rows(ortho, projected * weight_rows)
    update = (mapped * weight_rows).astype(jnp.bfloat16)
    return (patient_terms, core_terms, update)

def solve_right(rhs, matrix):
    lower = jnp.linalg.cholesky(matrix)
    return jax.scipy.linalg.cho_solve((lower, True), rhs.T).T

def reference(visits, counts, patient_weight, phenotype_core, feature_factor, static_data, static_factor):
    rows = VIS_DEV
    identity = jnp.eye(R, dtype=jnp.float32)
    features_wide = feature_factor.astype(jnp.float32)

    def per_group(carry, inputs):
        block, group_counts, group_weight = inputs
        block_wide = block.astype(jnp.float32)
        projected = jnp.dot(block_wide, features_wide, precision=lax.Precision.HIGHEST)
        row_owner, block_owner = layout(group_counts, rows, 0)
        weight_rows = jnp.dot(row_owner, group_weight, precision=lax.Precision.HIGHEST)
        field = core_field(projected, weight_rows, phenotype_core)
        factor = polar_factor(block_grams(field, block_owner))
        patient_terms, core_terms, update = finish(field, projected, weight_rows, block_owner, row_owner, factor, phenotype_core)
        feature_terms = contract_rows(block_wide, update.astype(jnp.float32))
        return ((carry[0] + feature_terms, carry[1] + core_terms), patient_terms)
    start_carry = (jnp.zeros((J, R), jnp.float32), jnp.zeros((R, R), jnp.float32))
    stacked = (visits.reshape(N_PAT, rows, J), counts.reshape(N_PAT, PAT_DEV), patient_weight.reshape(N_PAT, PAT_DEV, R))
    (feature_terms, core_terms), patient_terms = lax.scan(per_group, start_carry, stacked)
    patient_terms = patient_terms.reshape(K, R)
    coupled = jnp.dot(static_data.astype(jnp.float32), static_factor.astype(jnp.float32), preferred_element_type=jnp.float32)
    static_terms = contract_rows(static_data.astype(jnp.float32), patient_weight)
    core_gram = contract_rows(phenotype_core, phenotype_core)
    weight_gram = contract_rows(patient_weight, patient_weight)
    feature_gram = lax.dot_general(feature_factor.astype(jnp.float32), feature_factor.astype(jnp.float32), (((0,), (0,)), ((), ())), preferred_element_type=jnp.float32)
    static_gram = lax.dot_general(static_factor.astype(jnp.float32), static_factor.astype(jnp.float32), (((0,), (0,)), ((), ())), preferred_element_type=jnp.float32)
    core_new = solve_right(core_terms, feature_gram * weight_gram + MU_RIDGE * identity)
    feature_new = solve_right(feature_terms, core_gram * weight_gram + MU_RIDGE * identity)
    patient_new = solve_right(patient_terms + coupled, core_gram * feature_gram + static_gram + MU_RIDGE * identity)
    static_new = solve_right(static_terms, weight_gram + MU_RIDGE * identity)
    return (core_new, feature_new, patient_new, static_new)
```

```python
import functools

import jax
import jax.numpy as jnp
from jax import lax
from jax.experimental import pallas as pl
from jax.experimental.pallas import tpu as pltpu
from jax.sharding import PartitionSpec as P

BLK = 128
NS_STEPS = 8
MU_RIDGE = 1.0
F32 = jnp.float32
BF16 = jnp.bfloat16
MESH = pl.DeviceIdType.MESH

NN = (((1,), (0,)), ((), ()))
NT = (((1,), (1,)), ((), ()))
TN = (((0,), (0,)), ((), ()))


def dg(a, b, dims):
    return lax.dot_general(a, b, dims, preferred_element_type=F32)


def split(x):
    hi = x.astype(BF16)
    return hi, (x - hi.astype(F32)).astype(BF16)


def dot3(a, b, dims=NN):
    a_hi, a_lo = split(a)
    b_hi, b_lo = split(b)
    return dg(a_hi, b_hi, dims) + (dg(a_hi, b_lo, dims) + dg(a_lo, b_hi, dims))


def exact(a, b, dims=NN):
    return lax.dot_general(
        a, b, dims, precision=lax.Precision.HIGHEST, preferred_element_type=F32
    )


def solve(rhs, matrix, inverse):
    guess = dot3(rhs, inverse)
    return guess + dot3(rhs - exact(guess, matrix), inverse)


def kernel(
    n_pat, n_feat, chunks, tiles,
    counts, visits, weight, core, factor_in, static_data, static_factor,
    core_new, feature_new, patient_new, static_new,
    vis, proj, part, low_in, high_in, total,
    gram_out, gram_low, gram_high, gram_total, weights_all, static_all,
    mats, inverses, wides, row_weights, squares, grams, factors, halves, updates,
    terms_out, terms_in, core_out, core_in, new_out, new_in, coreg_out, coreg_in,
    vis_sem, part_send, low_recv, high_recv, total_send, total_recv,
    gram_sem, weight_send, weight_recv, static_send, static_recv,
    terms_send, terms_recv, core_send, core_recv,
    new_send, new_recv, coreg_send, coreg_recv,
):
    me = lax.axis_index("pat")
    z = lax.axis_index("feat")
    rank = core.shape[0]
    rows = visits.shape[0]
    rows_chunk = rows // chunks
    patients = weight.shape[0]
    features = visits.shape[1]
    piece = features // n_pat
    owners, core_rows = core_out.shape[0], core_out.shape[1]
    inner = z > 0
    outer = z < n_feat - 1

    def remote(src, dst, send, recv, **where):
        return pltpu.make_async_remote_copy(
            src_ref=src, dst_ref=dst, send_sem=send, recv_sem=recv,
            device_id=where, device_id_type=MESH,
        )

    def span(c):
        return pl.ds(pl.multiple_of(c * rows_chunk, rows_chunk), rows_chunk)

    def load(c):
        return pltpu.make_async_copy(visits.at[span(c)], vis.at[span(c)], vis_sem.at[c])

    @pl.loop(0, chunks)
    def _(c):
        load(c).start()

    barrier = pltpu.get_barrier_semaphore()
    for d in range(1, n_pat):
        pl.semaphore_signal(
            barrier, inc=1, device_id={"pat": lax.rem(me + d, n_pat)}, device_id_type=MESH
        )

    @pl.when(inner)
    def _():
        pl.semaphore_signal(barrier, inc=1, device_id={"feat": z - 1}, device_id_type=MESH)

    @pl.when(outer)
    def _():
        pl.semaphore_signal(barrier, inc=1, device_id={"feat": z + 1}, device_id_type=MESH)

    weights_all[me] = weight[...]
    static_all[me] = static_data[...].astype(F32)
    gram_own = jnp.concatenate(
        [
            dg(factor_in[...], factor_in[...], TN),
            dg(static_factor[...], static_factor[...], TN),
            dg(static_data[...], static_factor[...], NN),
        ],
        axis=0,
    )
    gram_out[...] = gram_own

    pl.semaphore_wait(
        barrier, n_pat - 1 + jnp.where(inner, 1, 0) + jnp.where(outer, 1, 0)
    )

    def gram_part(up):
        if up:
            return remote(gram_out, gram_low, gram_sem.at[0], gram_sem.at[1], feat=z + 1)
        return remote(gram_out, gram_high, gram_sem.at[0], gram_sem.at[2], feat=z - 1)

    def gram_back(up):
        return remote(
            gram_total, gram_total, gram_sem.at[4 if up else 3], gram_sem.at[5],
            feat=z + 1 if up else z - 1,
        )

    gram_owner = n_feat // 2

    @pl.when(z == 0)
    def _():
        gram_part(True).start()

    @pl.when(z == n_feat - 1)
    def _():
        gram_part(False).start()

    def weight_copy(d):
        peer = lax.rem(me + d, n_pat)
        return remote(
            weights_all.at[me], weights_all.at[me], weight_send.at[d], weight_recv.at[me], pat=peer
        )

    def static_copy(d):
        peer = lax.rem(me + d, n_pat)
        return remote(
            static_all.at[me], static_all.at[me], static_send.at[d], static_recv.at[me], pat=peer
        )

    for d in range(1, n_pat):
        weight_copy(d).start()
        static_copy(d).start()

    def owner_of(c):
        return n_feat // 2 - 1 + lax.rem(c, 2)

    def part_copy(c, up):
        if up:
            return remote(
                part.at[span(c)], low_in.at[span(c)], part_send.at[c], low_recv.at[c], feat=z + 1
            )
        return remote(
            part.at[span(c)], high_in.at[span(c)], part_send.at[c], high_recv.at[c], feat=z - 1
        )

    def total_copy(c, up):
        return remote(
            total.at[span(c)], total.at[span(c)], total_send.at[1 if up else 0, c],
            total_recv.at[c], feat=z + 1 if up else z - 1,
        )

    @pl.loop(0, chunks)
    def _(c):
        load(c).wait()
        product = dg(vis[span(c), :], factor_in[...], NN)
        proj[span(c), :] = product

        @pl.when(z == 0)
        def _():
            part[span(c), :] = product
            part_copy(c, True).start()

        @pl.when(z == n_feat - 1)
        def _():
            part[span(c), :] = product
            part_copy(c, False).start()

    @pl.when(inner & (z < gram_owner))
    def _():
        gram_part(True).wait_recv()
        gram_out[...] += gram_low[...]
        gram_part(True).start()

    @pl.when(outer & (z > gram_owner))
    def _():
        gram_part(False).wait_recv()
        gram_out[...] += gram_high[...]
        gram_part(False).start()

    @pl.when(z == gram_owner)
    def _():
        gram_part(True).wait_recv()
        gram_part(False).wait_recv()
        gram_total[...] = gram_out[...] + gram_low[...] + gram_high[...]
        gram_back(False).start()
        gram_back(True).start()

    def relay(c):
        owner = owner_of(c)

        @pl.when(inner & (z < owner))
        def _():
            part_copy(c, True).wait_recv()
            part[span(c), :] = proj[span(c), :] + low_in[span(c), :]
            part_copy(c, True).start()

        @pl.when(outer & (z > owner))
        def _():
            part_copy(c, False).wait_recv()
            part[span(c), :] = proj[span(c), :] + high_in[span(c), :]
            part_copy(c, False).start()

        @pl.when(z == owner)
        def _():
            part_copy(c, True).wait_recv()
            part_copy(c, False).wait_recv()
            total[span(c), :] = proj[span(c), :] + low_in[span(c), :] + high_in[span(c), :]
            total_copy(c, False).start()
            total_copy(c, True).start()

    def spread(c):
        owner = owner_of(c)

        @pl.when(z < owner)
        def _():
            total_copy(c, False).wait_recv()

            @pl.when(inner)
            def _():
                total_copy(c, False).start()

        @pl.when(z > owner)
        def _():
            total_copy(c, True).wait_recv()

            @pl.when(outer)
            def _():
                total_copy(c, True).start()

    lag = 4

    @pl.loop(0, lag)
    def _(c):
        relay(c)

    @pl.when(z < gram_owner)
    def _():
        gram_back(False).wait_recv()

        @pl.when(inner)
        def _():
            gram_back(False).start()

    @pl.when(z > gram_owner)
    def _():
        gram_back(True).wait_recv()

        @pl.when(outer)
        def _():
            gram_back(True).start()

    for d in range(1, n_pat):
        peer = lax.rem(me + d, n_pat)
        remote(
            weights_all.at[peer], weights_all.at[peer], weight_send.at[d], weight_recv.at[peer],
            pat=peer,
        ).wait_recv()
        remote(
            static_all.at[peer], static_all.at[peer], static_send.at[d], static_recv.at[peer],
            pat=peer,
        ).wait_recv()

    lane = lax.broadcasted_iota(jnp.int32, (rank, rank), 1)
    sub = lax.broadcasted_iota(jnp.int32, (rank, rank), 0)
    identity = (lane == sub).astype(F32)
    all_rows = weights_all[...].reshape(n_pat * patients, rank)
    weight_gram = exact(all_rows, all_rows, TN)
    core_gram = exact(core[...], core[...], TN)
    feature_gram = gram_total[pl.ds(0, rank), :]
    static_gram = gram_total[pl.ds(rank, rank), :]
    coupled = gram_total[pl.ds(2 * rank, patients), :]
    mats[0] = feature_gram * weight_gram + MU_RIDGE * identity
    mats[1] = core_gram * weight_gram + MU_RIDGE * identity
    mats[2] = core_gram * feature_gram + static_gram + MU_RIDGE * identity
    mats[3] = weight_gram + MU_RIDGE * identity
    inverses[...] = mats[...]

    lane_row = lax.broadcasted_iota(jnp.int32, (1, rank), 1)
    sub_col = lax.broadcasted_iota(jnp.int32, (rank, 1), 0)

    def eliminate(k):
        for m in range(4):
            whole = inverses[m]
            row = inverses[m, pl.ds(k, 1), :]
            pivot = jnp.sum(jnp.where(lane_row == k, row, 0.0), axis=1, keepdims=True)
            column = jnp.sum(jnp.where(lane == k, whole, 0.0), axis=1, keepdims=True)
            inverse = 1.0 / pivot
            scaled = jnp.where(lane_row == k, inverse, row * inverse)
            cleared = jnp.where((lane == k) | (sub == k), 0.0, whole)
            inverses[m] = cleared - jnp.where(sub_col == k, -1.0, column) * scaled

    share = rank // chunks

    def eliminate_some(c):
        @pl.loop(0, share)
        def _(j):
            eliminate(c * share + j)

    @pl.loop(lag, chunks)
    def _(c):
        relay(c)
        spread(c - lag)
        eliminate_some(c - lag)

    @pl.loop(chunks, chunks + lag)
    def _(c):
        spread(c - lag)
        eliminate_some(c - lag)

    blocks = rows // BLK
    group = 8
    starts, ends, lives = [], [], []
    position = jnp.int32(0)
    for k in range(patients):
        starts.append(position)
        lives.append(position + counts[k])
        position = position + ((counts[k] + (BLK - 1)) & (-BLK))
        ends.append(position)

    def coefficient(b, k):
        at = b * BLK
        return jnp.where((at >= starts[k]) & (at < ends[k]), 1.0, 0.0).astype(F32)

    start_row = jnp.full((1, rank), rows, jnp.int32)
    live_row = jnp.zeros((1, rank), jnp.int32)
    patient_col = lax.broadcasted_iota(jnp.int32, (patients, 1), 0)
    start_col = jnp.full((patients, 1), rows, jnp.int32)
    end_col = jnp.zeros((patients, 1), jnp.int32)
    for k in range(patients):
        start_row = jnp.where(lane_row == k, starts[k], start_row)
        live_row = jnp.where(lane_row == k, lives[k], live_row)
        start_col = jnp.where(patient_col == k, starts[k], start_col)
        end_col = jnp.where(patient_col == k, ends[k], end_col)
    weight_hi, weight_lo = split(
        jnp.concatenate([weight[...], jnp.zeros((rank - patients, rank), F32)], axis=0)
    )
    group_rows = group * BLK
    group_row = lax.broadcasted_iota(jnp.int32, (group_rows, rank), 0)

    def group_span(g):
        return pl.ds(pl.multiple_of(g * group_rows, group_rows), group_rows)

    @pl.loop(0, blocks // group)
    def _(g):
        at = group_row + g * group_rows
        live = jnp.where((at >= start_row) & (at < live_row), 1.0, 0.0).astype(BF16)
        by_row = dg(live, weight_hi, NN) + dg(live, weight_lo, NN)
        wide = total[group_span(g), :] * by_row
        row_weights[group_span(g), :] = by_row
        wides[group_span(g), :] = wide
        for i in range(group):
            one = wide[i * BLK : (i + 1) * BLK]
            squares[g * group + i] = dot3(one, one, TN)

    for k in range(patients):

        def add_blocks(g, acc, k=k):
            for i in range(group):
                b = g * group + i
                acc = acc + coefficient(b, k) * squares[b]
            return acc

        square = lax.fori_loop(0, blocks // group, add_blocks, jnp.zeros((rank, rank), F32))
        half = dot3(core[...], square)
        halves[k] = half
        gram = dot3(half, core[...], NT)
        trace = jnp.sum(jnp.sum(gram * identity, axis=1, keepdims=True), axis=0, keepdims=True)
        grams[k] = gram / trace
        factors[k] = identity / jnp.sqrt(trace)

    @pl.loop(0, NS_STEPS)
    def _(step):
        for k in range(patients):
            moment = grams[k]
            correction = 1.5 * identity - 0.5 * moment
            both = dot3(jnp.concatenate([factors[k], moment], axis=0), correction)
            factors[k] = both[:rank]
            grams[k] = dot3(correction, both[rank:])

    core_terms = jnp.zeros((rank, rank), F32)
    for k in range(patients):
        factor = factors[k]
        core_terms = core_terms + dot3(factor, halves[k], TN)
        grams[k] = dot3(core[...], dot3(factor, core[...]), TN)

    def core_copy(d):
        peer = lax.rem(me + d, n_pat)
        return remote(
            core_out.at[lax.rem(peer, owners)], core_in.at[me], core_send.at[d],
            core_recv.at[me], pat=peer,
        )

    core_out[...] = core_terms.reshape(owners, core_rows, rank)
    core_in[me] = core_out[lax.rem(me, owners)]
    for d in range(1, n_pat):
        core_copy(d).start()

    def map_group(g, sums):
        for i in range(group):
            b = g * group + i
            span_b = pl.ds(pl.multiple_of(b * BLK, BLK), BLK)
            mapper = coefficient(b, 0) * grams[0]
            for k in range(1, patients):
                mapper = mapper + coefficient(b, k) * grams[k]
            mapped = dot3(wides[span_b, :], mapper)
            products = mapped * total[span_b, :]
            updates[span_b, :] = (mapped * row_weights[span_b, :]).astype(BF16)
            at = b * BLK
            member = jnp.where((at >= start_col) & (at < end_col), 1.0, 0.0).astype(F32)
            sums = sums + member * jnp.sum(products, axis=0, keepdims=True)
        return sums

    patient_terms = lax.fori_loop(
        0, blocks // group, map_group, jnp.zeros((patients, rank), F32)
    )

    width = features // tiles
    per = n_pat // tiles

    def terms_copy(peer):
        return remote(
            terms_out.at[peer], terms_in.at[me], terms_send.at[peer], terms_recv.at[me], pat=peer
        )

    @pl.loop(0, tiles)
    def _(s):
        tile = lax.rem(lax.div(me, per) + 1 + s, tiles)
        columns = pl.ds(pl.multiple_of(tile * width, width), width)
        acc = jnp.zeros((width, rank), F32)
        for g in range(blocks // group):
            acc = acc + dg(
                vis[g * group_rows : (g + 1) * group_rows, columns],
                updates[g * group_rows : (g + 1) * group_rows, :],
                TN,
            )
        acc = solve(acc, mats[1], inverses[1]).astype(BF16)
        for j in range(per):
            peer = tile * per + j
            terms_out[peer] = acc[j * piece : (j + 1) * piece]

            @pl.when(peer != me)
            def _():
                terms_copy(peer).start()

    def each_peer(fn):
        for d in range(1, n_pat):
            fn(d, lax.rem(me + d, n_pat))

    def arrived(buffer, send, recv):
        def one(d, peer):
            remote(
                buffer.at[peer], buffer.at[peer], send.at[d], recv.at[peer], pat=peer
            ).wait_recv()

        each_peer(one)

    arrived(core_in, core_send, core_recv)
    terms_in[me] = terms_out[me]
    arrived(terms_in, terms_send, terms_recv)

    core_sum = jnp.sum(core_in[...], axis=0)
    coreg_out[...] = solve(core_sum, mats[0], inverses[0])
    terms_sum = jnp.sum(terms_in[...].astype(F32), axis=0)
    new_out[...] = terms_sum.astype(BF16)

    def new_copy(d):
        peer = lax.rem(me + d, n_pat)
        return remote(new_out, new_in.at[me], new_send.at[d], new_recv.at[me], pat=peer)

    def coreg_copy(d):
        peer = lax.rem(me + d, n_pat)
        return remote(coreg_out, coreg_in.at[me], coreg_send.at[d], coreg_recv.at[me], pat=peer)

    for d in range(1, n_pat):
        new_copy(d).start()
        coreg_copy(d).start()
    new_in[me] = new_out[...]
    coreg_in[me] = coreg_out[...]

    patient_new[...] = solve(
        patient_terms + coupled, mats[2], inverses[2]
    )
    static_terms = dot3(static_all[...].reshape(n_pat * patients, -1), all_rows, TN)
    static_new[...] = solve(static_terms, mats[3], inverses[3])

    arrived(coreg_in, coreg_send, coreg_recv)
    for q in range(owners):
        core_new[pl.ds(q * core_rows, core_rows), :] = coreg_in[q]
    arrived(new_in, new_send, new_recv)
    feature_new[...] = new_in[...].astype(F32).reshape(features, rank)

    for d in range(1, n_pat):
        weight_copy(d).wait_send()
        static_copy(d).wait_send()
        core_copy(d).wait_send()
        new_copy(d).wait_send()
        coreg_copy(d).wait_send()
        terms_copy(lax.rem(me + d, n_pat)).wait_send()

    @pl.when(z < gram_owner)
    def _():
        gram_part(True).wait_send()

        @pl.when(inner)
        def _():
            gram_back(False).wait_send()

    @pl.when(z > gram_owner)
    def _():
        gram_part(False).wait_send()

        @pl.when(outer)
        def _():
            gram_back(True).wait_send()

    @pl.when(z == gram_owner)
    def _():
        gram_back(False).wait_send()
        gram_back(True).wait_send()

    @pl.loop(0, chunks)
    def _(c):
        owner = owner_of(c)

        @pl.when(z < owner)
        def _():
            part_copy(c, True).wait_send()

            @pl.when(inner)
            def _():
                total_copy(c, False).wait_send()

        @pl.when(z > owner)
        def _():
            part_copy(c, False).wait_send()

            @pl.when(outer)
            def _():
                total_copy(c, True).wait_send()

        @pl.when(z == owner)
        def _():
            total_copy(c, False).wait_send()
            total_copy(c, True).wait_send()


def local(n_pat, n_feat, visits, counts, weight, core, factor, static_data, static_factor):
    rows, features = visits.shape
    patients, rank = weight.shape
    columns = static_data.shape[1]
    chunks = 16
    tiles = min(n_pat, features // 128)
    core_rows = max(rank // n_pat, 16)
    owners = rank // core_rows
    gram_rows = 2 * rank + patients
    piece = features // n_pat
    vmem, dma = pltpu.VMEM, pltpu.SemaphoreType.DMA
    scratch = [
        vmem((rows, features), BF16),
        vmem((rows, rank), F32),
        vmem((rows, rank), F32),
        vmem((rows, rank), F32),
        vmem((rows, rank), F32),
        vmem((rows, rank), F32),
        vmem((gram_rows, rank), F32),
        vmem((gram_rows, rank), F32),
        vmem((gram_rows, rank), F32),
        vmem((gram_rows, rank), F32),
        vmem((n_pat, patients, rank), F32),
        vmem((n_pat, patients, columns), F32),
        vmem((4, rank, rank), F32),
        vmem((4, rank, rank), F32),
        vmem((rows, rank), F32),
        vmem((rows, rank), F32),
        vmem((rows // BLK, rank, rank), F32),
        vmem((patients, rank, rank), F32),
        vmem((patients, rank, rank), F32),
        vmem((patients, rank, rank), F32),
        vmem((rows, rank), BF16),
        vmem((n_pat, piece, rank), BF16),
        vmem((n_pat, piece, rank), BF16),
        vmem((owners, core_rows, rank), F32),
        vmem((n_pat, core_rows, rank), F32),
        vmem((piece, rank), BF16),
        vmem((n_pat, piece, rank), BF16),
        vmem((core_rows, rank), F32),
        vmem((n_pat, core_rows, rank), F32),
        dma((chunks,)),
        dma((chunks,)),
        dma((chunks,)),
        dma((chunks,)),
        dma((2, chunks)),
        dma((chunks,)),
        dma((6,)),
    ] + [dma((n_pat,))] * 12
    space = pl.BlockSpec(memory_space=pltpu.VMEM)
    return pl.pallas_call(
        functools.partial(kernel, n_pat, n_feat, chunks, tiles),
        out_shape=(
            jax.ShapeDtypeStruct((rank, rank), F32),
            jax.ShapeDtypeStruct((features, rank), F32),
            jax.ShapeDtypeStruct((patients, rank), F32),
            jax.ShapeDtypeStruct((columns, rank), F32),
        ),
        in_specs=[
            pl.BlockSpec(memory_space=pltpu.SMEM),
            pl.BlockSpec(memory_space=pl.ANY),
            space, space, space, space, space,
        ],
        out_specs=(space, space, space, space),
        scratch_shapes=scratch,
        compiler_params=pltpu.CompilerParams(
            collective_id=0, has_side_effects=True, vmem_limit_bytes=62 * 1024 * 1024
        ),
        name="sweep",
    )(counts, visits, weight, core, factor, static_data, static_factor)


def solution(mesh):
    return jax.shard_map(
        functools.partial(local, mesh.shape["pat"], mesh.shape["feat"]),
        mesh=mesh,
        in_specs=(
            P("pat", "feat"),
            P("pat"),
            P("pat", None),
            P(),
            P("feat", None),
            P("pat", "feat"),
            P("feat", None),
        ),
        out_specs=(P(), P("feat", None), P("pat", None), P("feat", None)),
        check_vma=False,
    )
```
